512 devices in a mesh: view: 8 (over z_lo), gz: 64 (over y, x, z_hi, core).
Axes of the slice: x: 4, y: 4, z: 16 (z_hi: 2, z_lo: 8; z = z_hi * 8 + z_lo), core: 2. Of those that a mesh axis runs over, the one named last changes fastest.
Arguments:
- estimate: float32 [2048, 128, 128], P('gz'), may hold values from 0.25 to 4
- raw_bricks: bfloat16 [8, 32768, 4, 2, 128], P('view', 'gz'), may hold values from 0.25 to 4
- brick_slab: int32 [8, 32768, 1], P('view', 'gz'), may hold values from 0 to 63; in each aligned block of 512 rows (0 to 511, 512 to 1023, ..., all dimensions but the last counted through in order) at most 16 rows name the same one
- brick_pos: int32 [8, 32768], P('view', 'gz'), may hold values from 0 to 511
- off_z: int32 [8, 4], P('view'), may hold values from -1 to 3
- frac_z: float32 [8, 4], P('view'), may hold values from 0 to 1
- off_y: int32 [8, 2], P('view'), may hold values from -1 to 1
- frac_y: float32 [8, 2], P('view'), may hold values from 0 to 1
- off_x: int32 [8, 128], P('view'), may hold values from -1 to 127
- frac_x: float32 [8, 128], P('view'), may hold values from 0 to 1
- psf_z: float32 [8, 64], P('view'), may hold values from 0.05 to 1
- psf_y: float32 [8, 16], P('view'), may hold values from 0.05 to 1
- psf_x: float32 [8, 16], P('view'), may hold values from 0.05 to 1
Outputs:
- new_estimate: float32 [2048, 128, 128], P('gz', 'view')
The draws below stay inside these ranges and needn't reach their ends.
Inputs may be any that keep to these rules, and one draw needn't show every extreme that they name: `brick_slab`: in every view, the 512 bricks held by one device (an aligned block) name any one slab at most 16 times, a bound that some block reaches.
All inputs are finite; a program needn't handle non-finite values.
Results may differ from the reference program's by a relative error of at most 0.00043.
Values may be sent and summed in bfloat16 or wider, within the bound.
No kernel may reach another device: no remote copies, remote signals or barrier semaphores. Data moves between devices by JAX's collectives and lax.ppermute only.
A program may use at most 64 MiB of HBM per device.

```python
import math
import jax
import jax.numpy as jnp
import numpy as np
from jax import lax

CZ = 32
NY = 128
NX = 128
KZ = 64
KXY = 16
BZ = 4
BY = 2
VIEWS = 8
NZ = 2048
BPD = 512
BRICKS = 32768
CAP = 16
POS = 512
N_GZ = 64


def place_ends(entries, key, low, high):
    spot = [jax.random.randint(jax.random.fold_in(key, axis), (), 0, length) for axis, length in enumerate(entries.shape)]
    main_axis = entries.shape.index(max(entries.shape))
    beside = spot[:main_axis] + [(spot[main_axis] + 1) % entries.shape[main_axis]] + spot[main_axis + 1:]
    return entries.at[tuple(spot)].set(low).at[tuple(beside)].set(high)


def block_levels(stream_key, dims, cuts, smallest, high):
    level = 1.0
    for axis_at, parts in cuts:
        heights = jax.random.uniform(jax.random.fold_in(jax.random.fold_in(stream_key, 6), axis_at), (parts,), jnp.float32, smallest / len(cuts), high / len(cuts))
        level = level * jnp.repeat(jnp.exp(heights), dims[axis_at] // parts).reshape((-1,) + (1,) * (len(dims) - 1 - axis_at))
    return level


def deal_out(stream_key, own, number, rows, amount, top, reach, skew):
    sequence = jax.random.permutation(stream_key, amount)
    packed, usual = shares(amount, rows * top, reach, skew, True), shares(amount, rows * top, reach, skew, False)
    places = jnp.arange(amount)

    def named(tallies, rotation):
        used = int((tallies > 0).sum())
        fixed = max(1, used // 4)
        moved = fixed + (places - fixed + rotation * (used - fixed)) % max(1, amount - fixed)
        return jnp.zeros((amount,), jnp.int32).at[sequence[jnp.where(places < fixed, places, moved)]].set(jnp.asarray(tallies, jnp.int32))

    tallies = jnp.where(number % 4 == 0, named(packed, number // 4), named(usual, number - number // 4 - 1))
    mixed = jax.random.permutation(jax.random.fold_in(own, 3), amount)
    giver, sink = mixed[0:amount // 2 * 2:2], mixed[1:amount // 2 * 2:2]
    margin = jnp.minimum(tallies[giver] - 1, reach - tallies[sink]) // 2
    margin = jnp.where((giver == sequence[0]) | (sink == sequence[0]) | (tallies[sink] == 0), 0, jnp.maximum(margin, 0))
    moved = jax.random.randint(jax.random.fold_in(own, 4), (amount // 2,), 0, 1 << 20) % (margin + 1)
    tallies = tallies.at[giver].add(-moved).at[sink].add(moved)
    labels = jnp.searchsorted(jnp.cumsum(tallies), jnp.arange(rows * top), side="right").astype(jnp.int32)
    grid = labels.reshape(top, rows).T
    grid = grid[jax.random.permutation(jax.random.fold_in(own, 1), rows)]
    rotation = jax.random.randint(jax.random.fold_in(own, 2), (rows, 1), 0, top)
    return jnp.take_along_axis(grid, (jnp.arange(top)[None, :] + rotation) % top, axis=1)


def shares(number_of, total, reach, lean, full):
    loads = [(1 << 20) // math.isqrt(standing ** lean) + 1 for standing in range(1, number_of + 1)]
    largest = reach if full else min(reach, max(-(-total // number_of), total * loads[0] // sum(loads)))
    least = 1 if total - largest >= number_of - 1 else 0
    holding, rest = [largest] + [least] * (number_of - 1), total - largest - least * (number_of - 1)
    while rest > 0:
        free = [i for i in range(1, number_of) if holding[i] < largest] or [i for i in range(1, number_of) if holding[i] < reach]
        mass, budget = sum([loads[i] for i in free]), rest
        for i in free:
            extra = min(reach - holding[i], max(1, budget * loads[i] // mass), rest)
            holding[i] = holding[i] + extra
            rest = rest - extra
    return np.array(holding)


def setup_inputs(seed: int = 0) -> dict:
    splits = jax.random.split(jax.random.key(seed), 14)
    estimate = jnp.clip(jnp.exp(math.log(4.0) - 2.7725887 * jax.random.uniform(splits[0], (NZ, NY, NX), jnp.float32) ** block_levels(splits[0], (NZ, NY, NX), ((0, 64),), -0.2, 0.2)), 0.25, 4.0)
    raw_bricks = jnp.clip(jnp.exp(math.log(4.0) - 2.7725887 * jax.random.uniform(splits[1], (VIEWS, BRICKS, BZ, BY, NX), jnp.float32) ** block_levels(splits[1], (VIEWS, BRICKS, BZ, BY, NX), ((0, 8), (1, 64)), -0.2, 0.2)), 0.25, 4.0).astype(jnp.bfloat16)
    brick_slab_keys = jax.random.split(jax.random.fold_in(splits[2], 1), VIEWS * BRICKS // BPD)
    brick_slab_turns = jax.random.permutation(jax.random.fold_in(splits[2], 3), VIEWS * BRICKS // BPD)
    brick_slab = jax.vmap(lambda own, number: deal_out(jax.random.fold_in(splits[2], 2), own, number, BPD, N_GZ, 1, CAP, 2))(brick_slab_keys, brick_slab_turns).reshape((VIEWS, BRICKS, 1))
    brick_pos = place_ends(jax.random.randint(splits[3], (VIEWS, BRICKS), 0, POS), jax.random.fold_in(splits[3], 1), 0, POS - 1).astype(jnp.int32)
    off_z = place_ends(jax.random.randint(splits[4], (VIEWS, BZ), -1, BZ), jax.random.fold_in(splits[4], 1), -1, BZ - 1).astype(jnp.int32)
    frac_z = jnp.clip(1.0 * jax.random.uniform(splits[5], (VIEWS, BZ), jnp.float32) ** block_levels(splits[5], (VIEWS, BZ), ((0, 8),), -0.2, 0.2), 0.0, 1.0)
    off_y = place_ends(jax.random.randint(splits[6], (VIEWS, BY), -1, BY), jax.random.fold_in(splits[6], 1), -1, BY - 1).astype(jnp.int32)
    frac_y = jnp.clip(1.0 * jax.random.uniform(splits[7], (VIEWS, BY), jnp.float32) ** block_levels(splits[7], (VIEWS, BY), ((0, 8),), -0.2, 0.2), 0.0, 1.0)
    off_x = place_ends(jax.random.randint(splits[8], (VIEWS, NX), -1, NX), jax.random.fold_in(splits[8], 1), -1, NX - 1).astype(jnp.int32)
    frac_x = jnp.clip(1.0 * jax.random.uniform(splits[9], (VIEWS, NX), jnp.float32) ** block_levels(splits[9], (VIEWS, NX), ((0, 8),), -0.2, 0.2), 0.0, 1.0)
    psf_z = jnp.clip(jnp.exp(math.log(1.0) - 2.9957323 * jax.random.uniform(splits[10], (VIEWS, KZ), jnp.float32) ** block_levels(splits[10], (VIEWS, KZ), ((0, 8),), -0.2, 0.2)), 0.05, 1.0)
    psf_y = jnp.clip(jnp.exp(math.log(1.0) - 2.9957323 * jax.random.uniform(splits[11], (VIEWS, KXY), jnp.float32) ** block_levels(splits[11], (VIEWS, KXY), ((0, 8),), -0.2, 0.2)), 0.05, 1.0)
    psf_x = jnp.clip(jnp.exp(math.log(1.0) - 2.9957323 * jax.random.uniform(splits[12], (VIEWS, KXY), jnp.float32) ** block_levels(splits[12], (VIEWS, KXY), ((0, 8),), -0.2, 0.2)), 0.05, 1.0)
    return dict(estimate=estimate, raw_bricks=raw_bricks, brick_slab=brick_slab, brick_pos=brick_pos, off_z=off_z, frac_z=frac_z, off_y=off_y, frac_y=frac_y, off_x=off_x, frac_x=frac_x, psf_z=psf_z, psf_y=psf_y, psf_x=psf_x)


def rounded(values):
    return lax.optimization_barrier(values.astype(jnp.bfloat16)).astype(jnp.float32)


def weight_table(offsets, fractions, length):
    source_rows = jnp.arange(length, dtype=jnp.int32)[:, None]
    low_weight = rounded(1.0 - fractions)[None, :]
    high_weight = rounded(fractions)[None, :]
    table = jnp.where(source_rows == offsets[None, :], low_weight, jnp.float32(0.0))
    return table + jnp.where(source_rows == offsets[None, :] + 1, high_weight, jnp.float32(0.0))


def shifted_sum(padded, taps, axis, starts, length):
    result = None
    for tap_index in range(len(starts)):
        piece = taps[tap_index] * lax.slice_in_dim(padded, starts[tap_index], starts[tap_index] + length, axis=axis)
        result = piece if result is None else result + piece
    return result


def reference(estimate, raw_bricks, brick_slab, brick_pos, off_z, frac_z, off_y, frac_y, off_x, frac_x, psf_z, psf_y, psf_x):
    estimate_b = rounded(estimate)
    block_rows = NY // BY
    half_z = KZ // 2
    half_lat = KXY // 2

    def add_view(view, running):
        bricks = raw_bricks[view].astype(jnp.float32)
        offsets_x = off_x[view]
        fractions_x = frac_x[view]
        padded_x = jnp.pad(bricks, ((0, 0), (0, 0), (0, 0), (1, 1)))
        along_x = rounded(1.0 - fractions_x) * jnp.take(padded_x, offsets_x + 1, axis=3)
        along_x = along_x + rounded(fractions_x) * jnp.take(padded_x, offsets_x + 2, axis=3)
        along_x = rounded(along_x)
        table_z = weight_table(off_z[view], frac_z[view], BZ)
        table_y = weight_table(off_y[view], frac_y[view], BY)
        table_zy = rounded(jnp.einsum("ac,bd->abcd", table_z, table_y).reshape(BZ * BY, BZ * BY))
        mixed = jnp.einsum("qp,nqx->npx", table_zy, along_x.reshape(BRICKS, BZ * BY, NX))
        mixed = rounded(mixed)
        slab_ids = brick_slab[view, :, 0]
        places = brick_pos[view]
        block_z = (slab_ids * (CZ // BZ) + places // block_rows).astype(jnp.int32)
        block_y = (places % block_rows).astype(jnp.int32)
        blocks = jnp.zeros((NZ // BZ, block_rows, BZ, BY, NX), jnp.float32)
        blocks = blocks.at[block_z, block_y].add(mixed.reshape(BRICKS, BZ, BY, NX))
        joined = 1.0 + blocks.transpose(0, 2, 1, 3, 4).reshape(NZ, NY, NX)
        taps_z = rounded(psf_z[view] / jnp.sum(psf_z[view]))
        taps_y = rounded(psf_y[view] / jnp.sum(psf_y[view]))
        taps_x = rounded(psf_x[view] / jnp.sum(psf_x[view]))
        padded = jnp.pad(estimate_b, ((half_z, half_z), (0, 0), (0, 0)))
        blur_z = rounded(shifted_sum(padded, taps_z, 0, list(range(KZ)), NZ))
        padded = jnp.pad(blur_z, ((0, 0), (half_lat, KXY - 1 - half_lat), (0, 0)))
        blur_y = rounded(shifted_sum(padded, taps_y, 1, list(range(KXY)), NY))
        padded = jnp.pad(blur_y, ((0, 0), (0, 0), (half_lat, KXY - 1 - half_lat)))
        blurred = shifted_sum(padded, taps_x, 2, list(range(KXY)), NX)
        ratio = rounded(joined / blurred)
        padded = jnp.pad(ratio, ((half_z, half_z), (0, 0), (0, 0)))
        back_z = rounded(shifted_sum(padded, taps_z, 0, [2 * half_z - tap_index for tap_index in range(KZ)], NZ))
        padded = jnp.pad(back_z, ((0, 0), (KXY - 1 - half_lat, half_lat), (0, 0)))
        back_y = rounded(shifted_sum(padded, taps_y, 1, [KXY - 1 - tap_index for tap_index in range(KXY)], NY))
        padded = jnp.pad(back_y, ((0, 0), (0, 0), (KXY - 1 - half_lat, half_lat)))
        correction = shifted_sum(padded, taps_x, 2, [KXY - 1 - tap_index for tap_index in range(KXY)], NX)
        return running + correction

    total = lax.fori_loop(0, VIEWS, add_view, jnp.zeros((NZ, NY, NX), jnp.float32))
    return estimate * total / VIEWS
```

```python
import functools

import jax
import jax.numpy as jnp
from jax import lax
from jax.experimental import pallas as pl
from jax.experimental.pallas import tpu as pltpu
from jax.sharding import Mesh
from jax.sharding import PartitionSpec as P

BF = jnp.bfloat16
F32 = jnp.float32
I32 = jnp.int32
VMEM = pltpu.VMEM
SMEM = pltpu.SMEM


def iota(shape, dim):
    return lax.broadcasted_iota(I32, shape, dim)


def mm(a, b):
    return jnp.dot(a, b, preferred_element_type=F32)


def mm_nt(a, b):
    return lax.dot_general(a, b, (((1,), (1,)), ((), ())), preferred_element_type=F32)


def pack_kernel(cap, groups, slab_ref, pos_ref, bricks_ref, out_ref):
    count, cells = bricks_ref.shape
    slots = out_ref.shape[0]
    slab = slab_ref[...]
    pos = pos_ref[...]
    slabs = groups * 4
    member = (iota((slabs, count), 0) == slab).astype(BF)
    before = (iota((count, count), 0) < iota((count, count), 1)).astype(BF)
    earlier = mm(member, before)
    order = jnp.sum(earlier * member.astype(F32), axis=0, keepdims=True).astype(I32)
    chip = lax.shift_right_logical(slab, 2)
    half = lax.bitwise_and(lax.shift_right_logical(slab, 1), 1)
    core = lax.bitwise_and(slab, 1)
    slot = ((chip * 2 + core) * 2 + half) * cap + order
    block = lax.shift_right_logical(pos, 6) + 1
    row = lax.bitwise_and(pos, 63)
    which = iota((128, count), 0)
    places = jnp.where(which == 0, block, jnp.where(which == 1, row, 0)).astype(F32).astype(BF)
    step = 128
    for at in range(0, slots, step):
        chosen = (iota((step, count), 0) + at == slot).astype(BF)
        out_ref[at : at + step, :cells] = mm(chosen, bricks_ref[...]).astype(BF)
        out_ref[at : at + step, cells:] = mm_nt(chosen, places).astype(BF)


def pack(slab, pos, bricks, cap, groups):
    count, cells = bricks.shape
    slots = groups * 4 * cap
    return pl.pallas_call(
        functools.partial(pack_kernel, cap, groups),
        out_shape=jax.ShapeDtypeStruct((slots, cells + 128), BF),
        in_specs=[pl.BlockSpec(memory_space=VMEM)] * 3,
        out_specs=pl.BlockSpec(memory_space=VMEM),
        cost_estimate=pl.CostEstimate(
            flops=2 * slots * count * cells, bytes_accessed=2 * (count + slots) * cells, transcendentals=0
        ),
        name="pack",
    )(slab, pos, bricks)


def smem_sum(ref):
    total = ref[0, 0]
    for k in range(1, ref.shape[1]):
        total = total + ref[0, k]
    return total


def tap_table(psf_ref, which_tap):
    table = jnp.zeros(which_tap.shape, F32)
    for k in range(psf_ref.shape[1]):
        table = jnp.where(which_tap == k, psf_ref[0, k], table)
    total = jnp.full(which_tap.shape, smem_sum(psf_ref), F32)
    return (table / total).astype(BF)


def z_table(psf_ref, core, depth, direction):
    rows, cols = 2 * depth, 5 * depth
    r, c = iota((rows, cols), 0), iota((rows, cols), 1)
    out_plane = (lax.div(r, depth) * 2 + core) * depth + lax.rem(r, depth)
    block = lax.div(c, depth)
    own = jnp.where(block == 1, core, core + 2)
    other = jnp.where(block == 3, 1 - core, 3 - core)
    slab = jnp.where(block == 0, 5 * core - 1, jnp.where(block <= 2, own, other))
    in_plane = slab * depth + lax.rem(c, depth)
    half = psf_ref.shape[1] // 2
    return tap_table(psf_ref, direction * (in_plane - out_plane) + half)


def split_row(y, rows):
    half = rows // 2
    return jnp.where(y < half, 2 * y, 2 * (y - half) + 1)


def along_z(table, own_ref, oth_ref, beside_ref, out_ref, pair=2):
    _, rows, depth, cols = own_ref.shape
    planes = 2 * depth

    def column(y):
        return jnp.concatenate(
            [beside_ref[y], own_ref[0, y], own_ref[1, y], oth_ref[0, y], oth_ref[1, y]], axis=0
        )

    unroll = 4

    def body(i, carry):
        for u in range(unroll):
            y = (i * unroll + u) * pair
            data = jnp.concatenate([column(y + n) for n in range(pair)], axis=1)
            res = mm(table, data)
            for n in range(pair):
                out_ref[pl.ds(y + n, planes, stride=rows), :] = res[:, n * cols : (n + 1) * cols]
        return carry

    lax.fori_loop(0, rows // (pair * unroll), body, 0)


def blur_kernel(core_ref, psf_z_ref, psf_y_ref, psf_x_ref, own_ref, oth_ref, beside_ref, out_ref, mid):
    _, rows, depth, cols = own_ref.shape
    core = core_ref[0, 0]
    table_z = z_table(psf_z_ref, core, depth, 1)
    lateral = psf_y_ref.shape[1] // 2
    shape = (rows, rows)
    table_y = tap_table(psf_y_ref, iota(shape, 1) - split_row(iota(shape, 0), rows) + lateral)
    shape = (cols, cols)
    table_x = tap_table(psf_x_ref, iota(shape, 0) - iota(shape, 1) + lateral)
    along_z(table_z, own_ref, oth_ref, beside_ref, mid)

    unroll = 4

    def body(i, carry):
        for u in range(unroll):
            z = (i * unroll + u) * 2
            at = pl.multiple_of(z * rows, 2 * rows)
            first = mid[pl.ds(at, rows), :].astype(BF)
            second = mid[pl.ds(at + rows, rows), :].astype(BF)
            both = mm(table_y, jnp.concatenate([first, second], axis=1)).astype(BF)
            out_ref[pl.ds(at, rows), :] = mm(both[:, :cols], table_x)
            out_ref[pl.ds(at + rows, rows), :] = mm(both[:, cols:], table_x)
        return carry

    lax.fori_loop(0, 2 * depth // (2 * unroll), body, 0)


def slab_flops(rows, depth, cols):
    return 2 * 2 * depth * rows * cols * (5 * depth + rows + cols)


def blur(core, psf_z, psf_y, psf_x, own, oth, beside):
    _, rows, depth, cols = own.shape
    return pl.pallas_call(
        blur_kernel,
        out_shape=jax.ShapeDtypeStruct((2 * depth * rows, cols), F32),
        in_specs=[pl.BlockSpec(memory_space=SMEM)] * 4 + [pl.BlockSpec(memory_space=VMEM)] * 3,
        out_specs=pl.BlockSpec(memory_space=VMEM),
        scratch_shapes=[pltpu.VMEM((2 * depth * rows, cols), F32)],
        cost_estimate=pl.CostEstimate(
            flops=slab_flops(rows, depth, cols),
            bytes_accessed=18 * depth * rows * cols,
            transcendentals=0,
        ),
        name="blur",
    )(core, psf_z, psf_y, psf_x, own, oth, beside)


def interpolation(off_ref, frac_ref, length):
    table = []
    for a in range(length):
        line = []
        for c in range(length):
            frac = frac_ref[0, c]
            low = jnp.where(off_ref[0, c] == a, 1.0 - frac, 0.0)
            high = jnp.where(off_ref[0, c] + 1 == a, frac, 0.0)
            line.append((low, high))
        table.append(line)
    return table


def rounded(value):
    return value.astype(BF).astype(F32)


def join_kernel(
    cap,
    off_z_ref,
    frac_z_ref,
    off_y_ref,
    frac_y_ref,
    off_x_ref,
    frac_x_ref,
    arrived_ref,
    blurred_ref,
    out_ref,
    mixed,
    ratio,
):
    sources, _, width = arrived_ref.shape
    cols = off_x_ref.shape[1]
    deep, high = off_z_ref.shape[1], off_y_ref.shape[1]
    cells = deep * high
    _, rows, depth, _ = out_ref.shape
    spots = rows // high
    blocks = depth // deep
    places = spots * blocks
    slots = sources * cap
    source = iota((cols, cols), 0)
    off_x = off_x_ref[...]
    frac_x = frac_x_ref[...]
    table_x = jnp.where(source == off_x, rounded(1.0 - frac_x), 0.0)
    table_x = table_x + jnp.where(source == off_x + 1, rounded(frac_x), 0.0)
    table_x = table_x.astype(BF)
    weights_z = interpolation(off_z_ref, frac_z_ref, deep)
    weights_y = interpolation(off_y_ref, frac_y_ref, high)

    def spread(pair):
        low, up = pair
        return rounded(jnp.full((8, cols), low, F32)) + rounded(jnp.full((8, cols), up, F32))

    wide_z = [[spread(p) for p in line] for line in weights_z]
    wide_y = [[spread(p) for p in line] for line in weights_y]
    lane = iota((8, 128), 1)
    decode = jnp.where(lane == 0, spots, jnp.where(lane == 1, 1, 0)).astype(F32).astype(BF)
    for h in range(2):
        data = arrived_ref[:, h * cap : (h + 1) * cap, :].reshape(slots, width)
        place = mm_nt(decode, data[:, cells * cols :])[:1, :].astype(I32) - spots
        for b in range(blocks):
            chosen = (iota((spots, slots), 0) + b * spots == place).astype(BF)
            placed = mm(chosen, data[:, : cells * cols])
            for c in range(deep):
                for d in range(high):
                    acc = jnp.zeros((spots, cols), F32)
                    for a in range(deep):
                        for e in range(high):
                            weight = rounded(wide_z[a][c] * wide_y[e][d])
                            tile = placed[:, (a * high + e) * cols : (a * high + e + 1) * cols]
                            acc = acc + jnp.tile(weight, (spots // 8, 1)) * tile
                    plane = h * depth + b * deep + c
                    at = plane * rows + d * spots
                    mixed[at : at + spots, :] = acc.astype(BF)

    step = 512

    def body(i, carry):
        at = pl.multiple_of(i * step, step)
        joined = 0.5 + mm(mixed[pl.ds(at, step), :], table_x)
        ratio[pl.ds(at, step), :] = joined / blurred_ref[pl.ds(at, step), :]
        return carry

    lax.fori_loop(0, 2 * depth * rows // step, body, 0)

    def turn(y, carry):
        for h in range(2):
            line = ratio[pl.ds(h * depth * rows + y, depth, stride=rows), :]
            out_ref[h, y] = line.astype(BF)
        return carry

    lax.fori_loop(0, rows, turn, 0, unroll=8)


def join(cap, rows, depth, off_z, frac_z, off_y, frac_y, off_x, frac_x, arrived, blurred):
    cols = off_x.shape[1]
    cells = off_z.shape[1] * off_y.shape[1]
    slots = arrived.shape[0] * cap
    points = 2 * depth * rows
    return pl.pallas_call(
        functools.partial(join_kernel, cap),
        out_shape=jax.ShapeDtypeStruct((2, rows, depth, cols), BF),
        in_specs=[pl.BlockSpec(memory_space=SMEM)] * 4 + [pl.BlockSpec(memory_space=VMEM)] * 4,
        out_specs=pl.BlockSpec(memory_space=VMEM),
        scratch_shapes=[pltpu.VMEM((points, cols), BF), pltpu.VMEM((points, cols), F32)],
        cost_estimate=pl.CostEstimate(
            flops=2 * 2 * points // cells * slots * cells * cols // 2,
            bytes_accessed=8 * points * cols,
            transcendentals=0,
        ),
        name="join",
    )(off_z, frac_z, off_y, frac_y, off_x, frac_x, arrived, blurred)


def back_kernel(core_ref, psf_z_ref, psf_y_ref, psf_x_ref, own_ref, oth_ref, beside_ref, out_ref, mid):
    _, rows, depth, cols = own_ref.shape
    views = out_ref.shape[1]
    share = rows // views
    core = core_ref[0, 0]
    table_z = z_table(psf_z_ref, core, depth, -1)
    lateral = psf_y_ref.shape[1] // 2
    shape = (rows, rows)
    table_y = tap_table(psf_y_ref, iota(shape, 0) - split_row(iota(shape, 1), rows) + lateral)
    shape = (cols, cols)
    table_x = tap_table(psf_x_ref, iota(shape, 1) - iota(shape, 0) + lateral)
    along_z(table_z, own_ref, oth_ref, beside_ref, mid)

    unroll = 4

    for h in range(2):

        def body(i, carry):
            for u in range(unroll):
                z = (i * unroll + u) * 2
                at = pl.multiple_of((h * depth + z) * rows, 2 * rows)
                first = mid[pl.ds(at, rows), :].astype(BF)
                second = mid[pl.ds(at + rows, rows), :].astype(BF)
                both = mm(table_y, jnp.concatenate([first, second], axis=1)).astype(BF)
                for n in range(2):
                    res = mm(both[:, n * cols : (n + 1) * cols], table_x)
                    for v in range(views):
                        out_ref[h, v, z + n] = res[v * share : (v + 1) * share, :]
            return carry

        lax.fori_loop(0, depth // (2 * unroll), body, 0)


def back(core, psf_z, psf_y, psf_x, own, oth, beside, views):
    _, rows, depth, cols = own.shape
    return pl.pallas_call(
        back_kernel,
        out_shape=jax.ShapeDtypeStruct((2, views, depth, rows // views, cols), F32),
        in_specs=[pl.BlockSpec(memory_space=SMEM)] * 4 + [pl.BlockSpec(memory_space=VMEM)] * 3,
        out_specs=pl.BlockSpec(memory_space=VMEM),
        scratch_shapes=[pltpu.VMEM((2 * depth * rows, cols), F32)],
        cost_estimate=pl.CostEstimate(
            flops=slab_flops(rows, depth, cols),
            bytes_accessed=18 * depth * rows * cols,
            transcendentals=0,
        ),
        name="back",
    )(core, psf_z, psf_y, psf_x, own, oth, beside)


PLANE = ("y", "x", "core")
RING = ("zh", "view")


def with_sides(own, chips):
    core = lax.axis_index("core")
    other = lax.ppermute(own, "core", [(0, 1), (1, 0)])
    end = lax.dynamic_index_in_dim(own, core, 0, keepdims=False)
    pairs = []
    for chip in range(chips):
        if chip + 1 < chips:
            pairs.append((chip * 2 + 1, chip * 2 + 2))
        if chip > 0:
            pairs.append((chip * 2, chip * 2 - 1))
    return other, lax.ppermute(end, PLANE, pairs)


def shards(
    chips,
    cap,
    estimate,
    raw_bricks,
    brick_slab,
    brick_pos,
    off_z,
    frac_z,
    off_y,
    frac_y,
    off_x,
    frac_x,
    psf_z,
    psf_y,
    psf_x,
):
    depth, rows, cols = estimate.shape
    count = raw_bricks.shape[1]
    views = lax.axis_size("view")
    share = rows // views
    core = lax.axis_index("core").astype(I32).reshape(1, 1)

    packed = pack(
        brick_slab.reshape(1, count), brick_pos, raw_bricks.reshape(count, -1), cap, chips
    )
    packed = packed.reshape(2 * chips, 2 * cap, -1)
    arrived = lax.all_to_all(packed, PLANE, split_axis=0, concat_axis=0, tiled=True)

    part = lax.dynamic_slice_in_dim(estimate, lax.axis_index("view") * share, share, 1)
    piece = part.astype(BF).transpose(1, 0, 2)
    own = lax.all_gather(piece, RING, axis=0, tiled=True).reshape(2, rows, depth, cols)
    blurred = blur(core, psf_z, psf_y, psf_x, own, *with_sides(own, chips))

    ratio = join(cap, rows, depth, off_z, frac_z, off_y, frac_y, off_x, frac_x, arrived, blurred)
    correction = back(core, psf_z, psf_y, psf_x, ratio, *with_sides(ratio, chips), views)
    correction = correction.reshape(2 * views, depth, share, cols)
    total = lax.psum_scatter(correction, RING, scatter_dimension=0, tiled=True)
    return part * total.reshape(depth, share, cols) / views


def solution(mesh):
    devices = mesh.devices
    views, slabs = devices.shape
    fine = Mesh(devices.reshape(views, 4, slabs // 16, 2, 2), ("view", "y", "x", "zh", "core"))
    gz = ("y", "x", "zh", "core")
    in_specs = (
        P(gz, None, None),
        P("view", gz, None, None, None),
        P("view", gz, None),
        P("view", gz),
    ) + (P("view", None),) * 9
    out_specs = P(gz, "view", None)
    return jax.shard_map(
        functools.partial(shards, slabs // 4, 16),
        mesh=fine,
        in_specs=in_specs,
        out_specs=out_specs,
        check_vma=False,
    )
```

```python
import functools

import jax
import jax.numpy as jnp
from jax import lax
from jax.experimental import pallas as pl
from jax.experimental.pallas import tpu as pltpu
from jax.sharding import Mesh
from jax.sharding import PartitionSpec as P


BF = jnp.bfloat16
F32 = jnp.float32
I32 = jnp.int32
VMEM = pltpu.VMEM
SMEM = pltpu.SMEM
MIB = 1 << 20


def iota(shape, dim):
    return lax.broadcasted_iota(I32, shape, dim)


def mm(a, b):
    return jnp.dot(a, b, preferred_element_type=F32)


def mm_nt(a, b):
    return lax.dot_general(a, b, (((1,), (1,)), ((), ())), preferred_element_type=F32)


def pack_kernel(cap, groups, slab_ref, pos_ref, bricks_ref, out_ref):
    count, cells = bricks_ref.shape
    slots = out_ref.shape[0]
    slab = slab_ref[...]
    pos = pos_ref[...]
    slabs = groups * 4
    member = (iota((slabs, count), 0) == slab).astype(BF)
    before = (iota((count, count), 0) < iota((count, count), 1)).astype(BF)
    earlier = mm(member, before)
    order = jnp.sum(earlier * member.astype(F32), axis=0, keepdims=True).astype(I32)
    chip = lax.shift_right_logical(slab, 2)
    half = lax.bitwise_and(lax.shift_right_logical(slab, 1), 1)
    core = lax.bitwise_and(slab, 1)
    slot = ((chip * 2 + core) * 2 + half) * cap + order
    block = lax.shift_right_logical(pos, 6) + 1
    row = lax.bitwise_and(pos, 63)
    which = iota((128, count), 0)
    places = jnp.where(which == 0, block, jnp.where(which == 1, row, 0)).astype(F32).astype(BF)
    step = 128
    for at in range(0, slots, step):
        chosen = (iota((step, count), 0) + at == slot).astype(BF)
        out_ref[at : at + step, :cells] = mm(chosen, bricks_ref[...]).astype(BF)
        out_ref[at : at + step, cells:] = mm_nt(chosen, places).astype(BF)


def pack(slab, pos, bricks, cap, groups):
    count, cells = bricks.shape
    slots = groups * 4 * cap
    return pl.pallas_call(
        functools.partial(pack_kernel, cap, groups),
        out_shape=jax.ShapeDtypeStruct((slots, cells + 128), BF),
        in_specs=[pl.BlockSpec(memory_space=VMEM)] * 3,
        out_specs=pl.BlockSpec(memory_space=VMEM),
        compiler_params=pltpu.CompilerParams(vmem_limit_bytes=16 * MIB),
        cost_estimate=pl.CostEstimate(
            flops=2 * slots * count * cells, bytes_accessed=2 * (count + slots) * cells, transcendentals=0
        ),
        name="pack",
    )(slab, pos, bricks)


def smem_sum(ref):
    total = ref[0, 0]
    for k in range(1, ref.shape[1]):
        total = total + ref[0, k]
    return total


def tap_table(psf_ref, which_tap):
    table = jnp.zeros(which_tap.shape, F32)
    for k in range(psf_ref.shape[1]):
        table = jnp.where(which_tap == k, psf_ref[0, k], table)
    total = jnp.full(which_tap.shape, smem_sum(psf_ref), F32)
    return (table / total).astype(BF)


def z_table(psf_ref, core, depth, direction):
    rows, cols = depth, 3 * depth
    r, c = iota((rows, cols), 0), iota((rows, cols), 1)
    side = (lax.div(c, depth) - 1) * (1 - 2 * core)
    distance = side * depth + lax.rem(c, depth) - r
    half = psf_ref.shape[1] // 2
    return tap_table(psf_ref, direction * distance + half)


def split_row(y, rows):
    half = rows // 2
    return jnp.where(y < half, 2 * y, 2 * (y - half) + 1)


def turn_kernel(view_ref, part_ref, out_ref):
    out_ref[...] = jnp.swapaxes(part_ref[...], 0, 1).astype(BF)


def turn(view, estimate, share):
    depth, _, cols = estimate.shape
    return pl.pallas_call(
        turn_kernel,
        out_shape=jax.ShapeDtypeStruct((share, depth, cols), BF),
        grid_spec=pltpu.PrefetchScalarGridSpec(
            num_scalar_prefetch=1,
            grid=(1,),
            in_specs=[pl.BlockSpec((depth, share, cols), lambda i, view: (0, view[0], 0))],
            out_specs=pl.BlockSpec((share, depth, cols), lambda i, view: (0, 0, 0)),
        ),
        cost_estimate=pl.CostEstimate(
            flops=0, bytes_accessed=6 * depth * share * cols, transcendentals=0
        ),
        name="turn",
    )(view, estimate)


def finish_kernel(views, view_ref, part_ref, total_ref, out_ref):
    out_ref[...] = part_ref[...] * jnp.swapaxes(total_ref[...], 0, 1) / views


def finish(view, estimate, total, views):
    share, depth, cols = total.shape
    return pl.pallas_call(
        functools.partial(finish_kernel, views),
        out_shape=jax.ShapeDtypeStruct((depth, share, cols), F32),
        grid_spec=pltpu.PrefetchScalarGridSpec(
            num_scalar_prefetch=1,
            grid=(1,),
            in_specs=[
                pl.BlockSpec((depth, share, cols), lambda i, view: (0, view[0], 0)),
                pl.BlockSpec((share, depth, cols), lambda i, view: (0, 0, 0)),
            ],
            out_specs=pl.BlockSpec((depth, share, cols), lambda i, view: (0, 0, 0)),
        ),
        compiler_params=pltpu.CompilerParams(vmem_limit_bytes=8 * MIB),
        cost_estimate=pl.CostEstimate(
            flops=0, bytes_accessed=12 * depth * share * cols, transcendentals=0
        ),
        name="finish",
    )(view, estimate, total)


def twice(table):
    zero = jnp.zeros_like(table)
    top = jnp.concatenate([table, zero], axis=1)
    return jnp.concatenate([top, jnp.concatenate([zero, table], axis=1)], axis=0)


def tables_kernel(
    core_ref, psf_z_ref, psf_y_ref, psf_x_ref, az_ref, ay_ref, ax_ref, bz_ref, by_ref, bx_ref
):
    rows, cols = ay_ref.shape[0], ax_ref.shape[0] // 2
    core = core_ref[0, 0]
    lateral = psf_y_ref.shape[1] // 2
    az_ref[...] = z_table(psf_z_ref, core, az_ref.shape[0], 1)
    bz_ref[...] = z_table(psf_z_ref, core, bz_ref.shape[0], -1)
    line, across = iota((rows, rows), 0), iota((rows, rows), 1)
    ay_ref[...] = tap_table(psf_y_ref, across - split_row(line, rows) + lateral)
    by_ref[...] = tap_table(psf_y_ref, line - split_row(across, rows) + lateral)
    line, across = iota((cols, cols), 0), iota((cols, cols), 1)
    ax_ref[...] = twice(tap_table(psf_x_ref, line - across + lateral))
    bx_ref[...] = twice(tap_table(psf_x_ref, across - line + lateral))


def tables(core, psf_z, psf_y, psf_x, depth, rows, cols):
    shapes = ((depth, 3 * depth), (rows, rows), (2 * cols, 2 * cols))
    return pl.pallas_call(
        tables_kernel,
        out_shape=[jax.ShapeDtypeStruct(shape, BF) for shape in shapes * 2],
        in_specs=[pl.BlockSpec(memory_space=SMEM)] * 4,
        out_specs=[pl.BlockSpec(memory_space=VMEM)] * 6,
        compiler_params=pltpu.CompilerParams(vmem_limit_bytes=4 * MIB),
        name="tables",
    )(core, psf_z, psf_y, psf_x)


def middle_kernel(
    core_ref,
    az_ref,
    ay_ref,
    ax_ref,
    by_ref,
    bx_ref,
    one_ref,
    own_ref,
    two_ref,
    joined_ref,
    out_ref,
    mid,
    even,
    odd,
    res,
):
    rows, depth, cols = out_ref.shape

    def column(y):
        return jnp.concatenate([one_ref[y], own_ref[y], two_ref[y]], axis=0)

    def axial(i, carry):
        y = pl.multiple_of(i * 8, 8)
        lines = []
        for n in range(0, 8, 2):
            both = mm(az_ref[...], jnp.concatenate([column(y + n), column(y + n + 1)], axis=1))
            lines += [both[:, :cols], both[:, cols:]]
        mid[:, pl.ds(y, 8), :] = jnp.swapaxes(jnp.stack(lines), 0, 1)
        return carry

    lax.fori_loop(0, rows // 8, axial, 0)

    def at(pair):
        return pl.ds(pl.multiple_of(pair * rows, rows), rows)

    def along_y(i, carry):
        for n in range(4):
            pair = i * 4 + n
            both = jnp.concatenate([mid[2 * pair], mid[2 * pair + 1]], axis=1).astype(BF)
            even[at(pair), :] = mm(ay_ref[...], both).astype(BF)
        return carry

    lax.fori_loop(0, depth // 8, along_y, 0)

    def divide(i, carry):
        pair = 2 * i
        here = pl.ds(pl.multiple_of(pair * rows, 2 * rows), 2 * rows)
        blurred = mm(even[here, :], ax_ref[...])
        left = jnp.concatenate([joined_ref[2 * pair], joined_ref[2 * pair + 2]], axis=0)
        right = jnp.concatenate([joined_ref[2 * pair + 1], joined_ref[2 * pair + 3]], axis=0)
        odd[here, :cols] = (left / blurred[:, :cols]).astype(BF)
        odd[here, cols:] = (right / blurred[:, cols:]).astype(BF)
        return carry

    lax.fori_loop(0, depth // 4, divide, 0)

    def along_y_back(i, carry):
        for n in range(4):
            pair = i * 4 + n
            even[at(pair), :] = mm(by_ref[...], odd[at(pair), :]).astype(BF)
        return carry

    lax.fori_loop(0, depth // 8, along_y_back, 0)

    def along_x_back(i, carry):
        here = pl.ds(pl.multiple_of(i * 4 * rows, 4 * rows), 4 * rows)
        both = mm(even[here, :], bx_ref[...])
        planes = []
        for n in range(4):
            planes += [both[n * rows : (n + 1) * rows, k * cols : (k + 1) * cols] for k in (0, 1)]
        z = pl.multiple_of(i * 8, 8)
        res[:, pl.ds(z, 8), :] = jnp.swapaxes(jnp.stack(planes), 0, 1)
        return carry

    lax.fori_loop(0, depth // 8, along_x_back, 0)
    out_ref[...] = res[...].astype(BF)


def middle(core, weights, one, own, two, joined):
    _, rows, depth, cols = own[0].shape
    slab = (None, rows, depth, cols)
    points = depth * rows * cols
    half = (depth * rows // 2, 2 * cols)
    return pl.pallas_call(
        middle_kernel,
        out_shape=jax.ShapeDtypeStruct((rows, depth, cols), BF),
        grid_spec=pltpu.PrefetchScalarGridSpec(
            num_scalar_prefetch=1,
            grid=(1,),
            in_specs=[pl.BlockSpec(w.shape, lambda i, core: (0, 0)) for w in weights]
            + [
                pl.BlockSpec(slab, lambda i, core, which=which: (which(core[0]), 0, 0, 0))
                for _, which in (one, own, two)
            ]
            + [pl.BlockSpec((depth, rows, cols), lambda i, core: (0, 0, 0))],
            out_specs=pl.BlockSpec((rows, depth, cols), lambda i, core: (0, 0, 0)),
            scratch_shapes=[
                pltpu.VMEM((depth, rows, cols), F32),
                pltpu.VMEM(half, BF),
                pltpu.VMEM(half, BF),
                pltpu.VMEM((rows, depth, cols), F32),
            ],
        ),
        compiler_params=pltpu.CompilerParams(vmem_limit_bytes=28 * MIB),
        cost_estimate=pl.CostEstimate(
            flops=2 * points * (3 * depth + 2 * rows + 2 * cols),
            bytes_accessed=12 * points,
            transcendentals=0,
        ),
        name="middle",
    )(core, *weights, one[0], own[0], two[0], joined)


def interpolation(off_ref, frac_ref, length):
    table = []
    for a in range(length):
        line = []
        for c in range(length):
            frac = frac_ref[0, c]
            low = jnp.where(off_ref[0, c] == a, 1.0 - frac, 0.0)
            high = jnp.where(off_ref[0, c] + 1 == a, frac, 0.0)
            line.append((low, high))
        table.append(line)
    return table


def rounded(value):
    return value.astype(BF).astype(F32)


def join_kernel(
    cap,
    core_ref,
    off_z_ref,
    frac_z_ref,
    off_y_ref,
    frac_y_ref,
    off_x_ref,
    frac_x_ref,
    arrived_ref,
    inner_ref,
    outer_ref,
    mixed,
):
    sources, _, width = arrived_ref.shape
    cols = off_x_ref.shape[1]
    deep, high = off_z_ref.shape[1], off_y_ref.shape[1]
    cells = deep * high
    depth, rows, _ = inner_ref.shape
    core = core_ref[0, 0]
    spots = rows // high
    blocks = depth // deep
    slots = sources * cap
    source = iota((cols, cols), 0)
    off_x = off_x_ref[...]
    frac_x = frac_x_ref[...]
    table_x = jnp.where(source == off_x, rounded(1.0 - frac_x), 0.0)
    table_x = table_x + jnp.where(source == off_x + 1, rounded(frac_x), 0.0)
    table_x = table_x.astype(BF)
    weights_z = interpolation(off_z_ref, frac_z_ref, deep)
    weights_y = interpolation(off_y_ref, frac_y_ref, high)

    def spread(pair):
        low, up = pair
        return rounded(jnp.full((8, cols), low, F32)) + rounded(jnp.full((8, cols), up, F32))

    wide_z = [[spread(p) for p in line] for line in weights_z]
    wide_y = [[spread(p) for p in line] for line in weights_y]
    lane = iota((8, 128), 1)
    decode = jnp.where(lane == 0, spots, jnp.where(lane == 1, 1, 0)).astype(F32).astype(BF)
    for out_ref, h in ((inner_ref, 1 - core), (outer_ref, core)):
        data = arrived_ref[:, pl.ds(pl.multiple_of(h * cap, cap), cap), :].reshape(slots, width)
        place = mm_nt(decode, data[:, cells * cols :])[:1, :].astype(I32) - spots
        for b in range(blocks):
            chosen = (iota((spots, slots), 0) + b * spots == place).astype(BF)
            placed = mm(chosen, data[:, : cells * cols])
            for c in range(deep):
                for d in range(high):
                    acc = jnp.zeros((spots, cols), F32)
                    for a in range(deep):
                        for e in range(high):
                            weight = rounded(wide_z[a][c] * wide_y[e][d])
                            tile = placed[:, (a * high + e) * cols : (a * high + e + 1) * cols]
                            acc = acc + jnp.tile(weight, (spots // 8, 1)) * tile
                    at = (b * deep + c) * rows + d * spots
                    mixed[at : at + spots, :] = acc.astype(BF)
        out_ref[...] = (0.5 + mm(mixed[...], table_x)).reshape(depth, rows, cols)


def join(cap, rows, depth, core, off_z, frac_z, off_y, frac_y, off_x, frac_x, arrived):
    cols = off_x.shape[1]
    slots = arrived.shape[0] * cap
    points = depth * rows
    return pl.pallas_call(
        functools.partial(join_kernel, cap),
        out_shape=[jax.ShapeDtypeStruct((depth, rows, cols), F32)] * 2,
        in_specs=[pl.BlockSpec(memory_space=SMEM)] * 5 + [pl.BlockSpec(memory_space=VMEM)] * 3,
        out_specs=[pl.BlockSpec(memory_space=VMEM)] * 2,
        scratch_shapes=[pltpu.VMEM((points, cols), BF)],
        compiler_params=pltpu.CompilerParams(vmem_limit_bytes=28 * MIB),
        cost_estimate=pl.CostEstimate(
            flops=2 * 2 * points * (slots + cols) * cols,
            bytes_accessed=12 * points * cols,
            transcendentals=0,
        ),
        name="join",
    )(core, off_z, frac_z, off_y, frac_y, off_x, frac_x, arrived)


def back_kernel(
    core_ref, table, beside_ref, outer_ref, oth_inner_ref, inner_ref, oth_outer_ref, out_ref
):
    share, _, cols = beside_ref.shape
    core = core_ref[0]
    for half, refs in (
        (core, (beside_ref, outer_ref, oth_inner_ref)),
        (1 - core, (oth_inner_ref, inner_ref, oth_outer_ref)),
    ):
        for n in range(0, share, 2):
            data = [jnp.concatenate([ref[n + k] for ref in refs], axis=0) for k in range(2)]
            both = mm(table[...], jnp.concatenate(data, axis=1))
            out_ref[half, n] = both[:, :cols]
            out_ref[half, n + 1] = both[:, cols:]


def back(core, table, beside, outer, oth_inner, inner, oth_outer, share):
    rows, depth, cols = outer.shape
    slab = pl.BlockSpec((share, depth, cols), lambda i, core: (i, 0, 0))
    points = 2 * depth * rows * cols
    return pl.pallas_call(
        back_kernel,
        out_shape=pltpu.HBM((2, rows, depth, cols), F32),
        grid_spec=pltpu.PrefetchScalarGridSpec(
            num_scalar_prefetch=1,
            grid=(rows // share,),
            in_specs=[pl.BlockSpec(table.shape, lambda i, core: (0, 0))] + [slab] * 5,
            out_specs=pl.BlockSpec((2, share, depth, cols), lambda i, core: (0, i, 0, 0)),
        ),
        compiler_params=pltpu.CompilerParams(vmem_limit_bytes=8 * MIB),
        cost_estimate=pl.CostEstimate(
            flops=2 * points * 3 * depth, bytes_accessed=9 * points, transcendentals=0
        ),
        name="back",
    )(core, table, beside, outer, oth_inner, inner, oth_outer)


PLANE = ("y", "x", "core")
RING = ("zh", "view")


def swapped(own):
    return lax.ppermute(own, "core", [(0, 1), (1, 0)])


def from_next(end, chips):
    pairs = []
    for chip in range(chips):
        if chip + 1 < chips:
            pairs.append((chip * 2 + 1, chip * 2 + 2))
        if chip > 0:
            pairs.append((chip * 2, chip * 2 - 1))
    return lax.ppermute(end, PLANE, pairs)


def shards(
    chips,
    cap,
    estimate,
    raw_bricks,
    brick_slab,
    brick_pos,
    off_z,
    frac_z,
    off_y,
    frac_y,
    off_x,
    frac_x,
    psf_z,
    psf_y,
    psf_x,
):
    depth, rows, cols = estimate.shape
    count = raw_bricks.shape[1]
    views = lax.axis_size("view")
    share = rows // views
    core = lax.axis_index("core").astype(I32)
    view = lax.axis_index("view").astype(I32)
    place = core.reshape(1)

    piece = turn(view.reshape(1), estimate, share)
    own = lax.all_gather(piece, RING, axis=0, tiled=True).reshape(2, rows, depth, cols)

    packed = pack(
        brick_slab.reshape(1, count), brick_pos, raw_bricks.reshape(count, -1), cap, chips
    )
    packed = packed.reshape(2 * chips, 2 * cap, -1)
    arrived = lax.all_to_all(packed, PLANE, split_axis=0, concat_axis=0, tiled=True)
    joined_inner, joined_outer = join(
        cap, rows, depth, core.reshape(1, 1), off_z, frac_z, off_y, frac_y, off_x, frac_x, arrived
    )

    end = lax.dynamic_index_in_dim(own, core, 0, keepdims=False)
    own, end = lax.optimization_barrier((own, end))
    beside = from_next(end, chips)[None]
    oth = swapped(own)
    az, ay, ax, bz, by, bx = tables(core.reshape(1, 1), psf_z, psf_y, psf_x, depth, rows, cols)
    weights = (az, ay, ax, by, bx)
    same, flip, first = (lambda c: c), (lambda c: 1 - c), (lambda c: 0)
    inner = middle(place, weights, (oth, same), (own, flip), (oth, flip), joined_inner)
    outer = middle(place, weights, (beside, first), (own, same), (oth, same), joined_outer)

    oth_inner = swapped(inner)
    beside = from_next(outer, chips)
    oth_outer = swapped(outer)
    correction = back(place, bz, beside, outer, oth_inner, inner, oth_outer, share)
    correction = correction.reshape(2 * views, share, depth, cols)
    total = lax.psum_scatter(correction, RING, scatter_dimension=0, tiled=True)
    return finish(view.reshape(1), estimate, total.reshape(share, depth, cols), views)


def solution(mesh):
    devices = mesh.devices
    views, slabs = devices.shape
    fine = Mesh(devices.reshape(views, 4, slabs // 16, 2, 2), ("view", "y", "x", "zh", "core"))
    gz = ("y", "x", "zh", "core")
    in_specs = (
        P(gz, None, None),
        P("view", gz, None, None, None),
        P("view", gz, None),
        P("view", gz),
    ) + (P("view", None),) * 9
    out_specs = P(gz, "view", None)
    return jax.shard_map(
        functools.partial(shards, slabs // 4, 16),
        mesh=fine,
        in_specs=in_specs,
        out_specs=out_specs,
        check_vma=False,
    )
```

```python
import functools

import jax
import jax.numpy as jnp
from jax import lax
from jax.experimental import pallas as pl
from jax.experimental.pallas import tpu as pltpu
from jax.sharding import Mesh
from jax.sharding import PartitionSpec as P


BF = jnp.bfloat16
F32 = jnp.float32
I32 = jnp.int32
VMEM = pltpu.VMEM
SMEM = pltpu.SMEM
MIB = 1 << 20


def iota(shape, dim):
    return lax.broadcasted_iota(I32, shape, dim)


def mm(a, b):
    return jnp.dot(a, b, preferred_element_type=F32)


def mm_nt(a, b):
    return lax.dot_general(a, b, (((1,), (1,)), ((), ())), preferred_element_type=F32)


def pack_kernel(cap, groups, slab_ref, pos_ref, bricks_ref, out_ref):
    count, cells = bricks_ref.shape
    slots = out_ref.shape[0]
    slab = slab_ref[...]
    pos = pos_ref[...]
    slabs = groups * 4
    member = (iota((slabs, count), 0) == slab).astype(BF)
    before = (iota((count, count), 0) < iota((count, count), 1)).astype(BF)
    earlier = mm(member, before)
    order = jnp.sum(earlier * member.astype(F32), axis=0, keepdims=True).astype(I32)
    chip = lax.shift_right_logical(slab, 2)
    half = lax.bitwise_and(lax.shift_right_logical(slab, 1), 1)
    core = lax.bitwise_and(slab, 1)
    slot = ((chip * 2 + core) * 2 + half) * cap + order
    block = lax.shift_right_logical(pos, 6) + 1
    row = lax.bitwise_and(pos, 63)
    which = iota((128, count), 0)
    places = jnp.where(which == 0, block, jnp.where(which == 1, row, 0)).astype(F32).astype(BF)
    step = 128
    for at in range(0, slots, step):
        chosen = (iota((step, count), 0) + at == slot).astype(BF)
        out_ref[at : at + step, :cells] = mm(chosen, bricks_ref[...]).astype(BF)
        out_ref[at : at + step, cells:] = mm_nt(chosen, places).astype(BF)


def pack(slab, pos, bricks, cap, groups):
    count, cells = bricks.shape
    slots = groups * 4 * cap
    return pl.pallas_call(
        functools.partial(pack_kernel, cap, groups),
        out_shape=jax.ShapeDtypeStruct((slots, cells + 128), BF),
        in_specs=[pl.BlockSpec(memory_space=VMEM)] * 3,
        out_specs=pl.BlockSpec(memory_space=VMEM),
        compiler_params=pltpu.CompilerParams(vmem_limit_bytes=16 * MIB),
        cost_estimate=pl.CostEstimate(
            flops=2 * slots * count * cells, bytes_accessed=2 * (count + slots) * cells, transcendentals=0
        ),
        name="pack",
    )(slab, pos, bricks)


def smem_sum(ref):
    total = ref[0, 0]
    for k in range(1, ref.shape[1]):
        total = total + ref[0, k]
    return total


def tap_table(psf_ref, which_tap):
    table = jnp.zeros(which_tap.shape, F32)
    for k in range(psf_ref.shape[1]):
        table = jnp.where(which_tap == k, psf_ref[0, k], table)
    total = jnp.full(which_tap.shape, smem_sum(psf_ref), F32)
    return (table / total).astype(BF)


def z_table(psf_ref, core, depth, direction):
    rows, cols = depth, 3 * depth
    r, c = iota((rows, cols), 0), iota((rows, cols), 1)
    side = (lax.div(c, depth) - 1) * (1 - 2 * core)
    distance = side * depth + lax.rem(c, depth) - r
    half = psf_ref.shape[1] // 2
    return tap_table(psf_ref, direction * distance + half)


def split_row(y, rows):
    half = rows // 2
    return jnp.where(y < half, 2 * y, 2 * (y - half) + 1)


def turn_kernel(view_ref, part_ref, out_ref):
    out_ref[...] = jnp.swapaxes(part_ref[...], 0, 1).astype(BF)


def turn(view, estimate, share):
    depth, _, cols = estimate.shape
    return pl.pallas_call(
        turn_kernel,
        out_shape=jax.ShapeDtypeStruct((share, depth, cols), BF),
        grid_spec=pltpu.PrefetchScalarGridSpec(
            num_scalar_prefetch=1,
            grid=(1,),
            in_specs=[pl.BlockSpec((depth, share, cols), lambda i, view: (0, view[0], 0))],
            out_specs=pl.BlockSpec((share, depth, cols), lambda i, view: (0, 0, 0)),
        ),
        cost_estimate=pl.CostEstimate(
            flops=0, bytes_accessed=6 * depth * share * cols, transcendentals=0
        ),
        name="turn",
    )(view, estimate)


def finish_kernel(views, view_ref, part_ref, total_ref, out_ref):
    out_ref[...] = part_ref[...] * jnp.swapaxes(total_ref[...], 0, 1) / views


def finish(view, estimate, total, views):
    share, depth, cols = total.shape
    return pl.pallas_call(
        functools.partial(finish_kernel, views),
        out_shape=jax.ShapeDtypeStruct((depth, share, cols), F32),
        grid_spec=pltpu.PrefetchScalarGridSpec(
            num_scalar_prefetch=1,
            grid=(1,),
            in_specs=[
                pl.BlockSpec((depth, share, cols), lambda i, view: (0, view[0], 0)),
                pl.BlockSpec((share, depth, cols), lambda i, view: (0, 0, 0)),
            ],
            out_specs=pl.BlockSpec((depth, share, cols), lambda i, view: (0, 0, 0)),
        ),
        cost_estimate=pl.CostEstimate(
            flops=0, bytes_accessed=12 * depth * share * cols, transcendentals=0
        ),
        name="finish",
    )(view, estimate, total)


def twice(table):
    zero = jnp.zeros_like(table)
    top = jnp.concatenate([table, zero], axis=1)
    return jnp.concatenate([top, jnp.concatenate([zero, table], axis=1)], axis=0)


def tables_kernel(
    core_ref, psf_z_ref, psf_y_ref, psf_x_ref, az_ref, ay_ref, ax_ref, bz_ref, by_ref, bx_ref
):
    rows, cols = ay_ref.shape[0], ax_ref.shape[0] // 2
    core = core_ref[0, 0]
    lateral = psf_y_ref.shape[1] // 2
    az_ref[...] = z_table(psf_z_ref, core, az_ref.shape[0], 1)
    bz_ref[...] = z_table(psf_z_ref, core, bz_ref.shape[0], -1)
    line, across = iota((rows, rows), 0), iota((rows, rows), 1)
    ay_ref[...] = tap_table(psf_y_ref, across - split_row(line, rows) + lateral)
    by_ref[...] = tap_table(psf_y_ref, line - split_row(across, rows) + lateral)
    line, across = iota((cols, cols), 0), iota((cols, cols), 1)
    ax_ref[...] = twice(tap_table(psf_x_ref, line - across + lateral))
    bx_ref[...] = twice(tap_table(psf_x_ref, across - line + lateral))


def tables(core, psf_z, psf_y, psf_x, depth, rows, cols):
    shapes = ((depth, 3 * depth), (rows, rows), (2 * cols, 2 * cols))
    return pl.pallas_call(
        tables_kernel,
        out_shape=[jax.ShapeDtypeStruct(shape, BF) for shape in shapes * 2],
        in_specs=[pl.BlockSpec(memory_space=SMEM)] * 4,
        out_specs=[pl.BlockSpec(memory_space=VMEM)] * 6,
        compiler_params=pltpu.CompilerParams(vmem_limit_bytes=4 * MIB),
        name="tables",
    )(core, psf_z, psf_y, psf_x)


def pick_kernel(core_ref, own_ref, out_ref):
    pltpu.sync_copy(own_ref.at[core_ref[0]], out_ref)


def pick(core, own):
    return pl.pallas_call(
        pick_kernel,
        out_shape=jax.ShapeDtypeStruct(own.shape[1:], own.dtype),
        in_specs=[pl.BlockSpec(memory_space=SMEM), pl.BlockSpec(memory_space=pltpu.HBM)],
        out_specs=pl.BlockSpec(memory_space=VMEM),
        compiler_params=pltpu.CompilerParams(vmem_limit_bytes=4 * MIB),
        cost_estimate=pl.CostEstimate(flops=0, bytes_accessed=2 * own.size, transcendentals=0),
        name="pick",
    )(core, own)


def middle_kernel(
    picks,
    core_ref,
    az_ref,
    ay_ref,
    ax_ref,
    by_ref,
    bx_ref,
    one_ref,
    own_ref,
    two_ref,
    joined_ref,
    out_ref,
    mid,
    even,
    odd,
    res,
):
    rows, depth, cols = out_ref.shape
    one_ref, two_ref = (
        ref.at[which(core_ref[0])] for ref, which in zip((one_ref, two_ref), picks, strict=True)
    )

    def column(y):
        return jnp.concatenate([one_ref[y], own_ref[y], two_ref[y]], axis=0)

    def axial(i, carry):
        y = pl.multiple_of(i * 8, 8)
        lines = []
        for n in range(0, 8, 2):
            both = mm(az_ref[...], jnp.concatenate([column(y + n), column(y + n + 1)], axis=1))
            lines += [both[:, :cols], both[:, cols:]]
        mid[:, pl.ds(y, 8), :] = jnp.swapaxes(jnp.stack(lines), 0, 1)
        return carry

    lax.fori_loop(0, rows // 8, axial, 0)

    def at(pair):
        return pl.ds(pl.multiple_of(pair * rows, rows), rows)

    def along_y(i, carry):
        for n in range(4):
            pair = i * 4 + n
            both = jnp.concatenate([mid[2 * pair], mid[2 * pair + 1]], axis=1).astype(BF)
            even[at(pair), :] = mm(ay_ref[...], both).astype(BF)
        return carry

    lax.fori_loop(0, depth // 8, along_y, 0)

    def divide(i, carry):
        pair = 2 * i
        here = pl.ds(pl.multiple_of(pair * rows, 2 * rows), 2 * rows)
        blurred = mm(even[here, :], ax_ref[...])
        left = jnp.concatenate([joined_ref[2 * pair], joined_ref[2 * pair + 2]], axis=0)
        right = jnp.concatenate([joined_ref[2 * pair + 1], joined_ref[2 * pair + 3]], axis=0)
        odd[here, :cols] = (left / blurred[:, :cols]).astype(BF)
        odd[here, cols:] = (right / blurred[:, cols:]).astype(BF)
        return carry

    lax.fori_loop(0, depth // 4, divide, 0)

    def along_y_back(i, carry):
        for n in range(4):
            pair = i * 4 + n
            even[at(pair), :] = mm(by_ref[...], odd[at(pair), :]).astype(BF)
        return carry

    lax.fori_loop(0, depth // 8, along_y_back, 0)

    def along_x_back(i, carry):
        here = pl.ds(pl.multiple_of(i * 4 * rows, 4 * rows), 4 * rows)
        both = mm(even[here, :], bx_ref[...])
        planes = []
        for n in range(4):
            planes += [both[n * rows : (n + 1) * rows, k * cols : (k + 1) * cols] for k in (0, 1)]
        z = pl.multiple_of(i * 8, 8)
        res[:, pl.ds(z, 8), :] = jnp.swapaxes(jnp.stack(planes), 0, 1)
        return carry

    lax.fori_loop(0, depth // 8, along_x_back, 0)
    out_ref[...] = res[...].astype(BF)


def middle(core, weights, one, own, two, joined):
    _, rows, depth, cols = own[0].shape
    points = depth * rows * cols
    half = (depth * rows // 2, 2 * cols)
    whole = pl.BlockSpec(memory_space=VMEM)
    own_spec = pl.BlockSpec((None, rows, depth, cols), lambda i, core: (own[1](core[0]), 0, 0, 0))
    return pl.pallas_call(
        functools.partial(middle_kernel, (one[1], two[1])),
        out_shape=jax.ShapeDtypeStruct((rows, depth, cols), BF),
        grid_spec=pltpu.PrefetchScalarGridSpec(
            num_scalar_prefetch=1,
            grid=(1,),
            in_specs=[whole] * (len(weights) + 1) + [own_spec] + [whole] * 2,
            out_specs=whole,
            scratch_shapes=[
                pltpu.VMEM((depth, rows, cols), F32),
                pltpu.VMEM(half, BF),
                pltpu.VMEM(half, BF),
                pltpu.VMEM((rows, depth, cols), F32),
            ],
        ),
        compiler_params=pltpu.CompilerParams(vmem_limit_bytes=20 * MIB),
        cost_estimate=pl.CostEstimate(
            flops=2 * points * (3 * depth + 2 * rows + 2 * cols),
            bytes_accessed=12 * points,
            transcendentals=0,
        ),
        name="middle",
    )(core, *weights, one[0], own[0], two[0], joined)


def interpolation(off_ref, frac_ref, length):
    table = []
    for a in range(length):
        line = []
        for c in range(length):
            frac = frac_ref[0, c]
            low = jnp.where(off_ref[0, c] == a, 1.0 - frac, 0.0)
            high = jnp.where(off_ref[0, c] + 1 == a, frac, 0.0)
            line.append((low, high))
        table.append(line)
    return table


def rounded(value):
    return value.astype(BF).astype(F32)


def join_kernel(
    cap,
    core_ref,
    off_z_ref,
    frac_z_ref,
    off_y_ref,
    frac_y_ref,
    off_x_ref,
    frac_x_ref,
    arrived_ref,
    inner_ref,
    outer_ref,
    mixed,
):
    sources, _, width = arrived_ref.shape
    cols = off_x_ref.shape[1]
    deep, high = off_z_ref.shape[1], off_y_ref.shape[1]
    cells = deep * high
    depth, rows, _ = inner_ref.shape
    core = core_ref[0, 0]
    spots = rows // high
    blocks = depth // deep
    slots = sources * cap
    source = iota((cols, cols), 0)
    off_x = off_x_ref[...]
    frac_x = frac_x_ref[...]
    table_x = jnp.where(source == off_x, rounded(1.0 - frac_x), 0.0)
    table_x = table_x + jnp.where(source == off_x + 1, rounded(frac_x), 0.0)
    table_x = table_x.astype(BF)
    weights_z = interpolation(off_z_ref, frac_z_ref, deep)
    weights_y = interpolation(off_y_ref, frac_y_ref, high)

    def spread(pair):
        low, up = pair
        return rounded(jnp.full((8, cols), low, F32)) + rounded(jnp.full((8, cols), up, F32))

    wide_z = [[spread(p) for p in line] for line in weights_z]
    wide_y = [[spread(p) for p in line] for line in weights_y]
    lane = iota((8, 128), 1)
    decode = jnp.where(lane == 0, spots, jnp.where(lane == 1, 1, 0)).astype(F32).astype(BF)
    for out_ref, h in ((inner_ref, 1 - core), (outer_ref, core)):
        data = arrived_ref[:, pl.ds(pl.multiple_of(h * cap, cap), cap), :].reshape(slots, width)
        place = mm_nt(decode, data[:, cells * cols :])[:1, :].astype(I32) - spots
        for b in range(blocks):
            chosen = (iota((spots, slots), 0) + b * spots == place).astype(BF)
            placed = mm(chosen, data[:, : cells * cols])
            for c in range(deep):
                for d in range(high):
                    acc = jnp.zeros((spots, cols), F32)
                    for a in range(deep):
                        for e in range(high):
                            weight = rounded(wide_z[a][c] * wide_y[e][d])
                            tile = placed[:, (a * high + e) * cols : (a * high + e + 1) * cols]
                            acc = acc + jnp.tile(weight, (spots // 8, 1)) * tile
                    at = (b * deep + c) * rows + d * spots
                    mixed[at : at + spots, :] = acc.astype(BF)
        out_ref[...] = (0.5 + mm(mixed[...], table_x)).reshape(depth, rows, cols)


def join(cap, rows, depth, core, off_z, frac_z, off_y, frac_y, off_x, frac_x, arrived):
    cols = off_x.shape[1]
    slots = arrived.shape[0] * cap
    points = depth * rows
    return pl.pallas_call(
        functools.partial(join_kernel, cap),
        out_shape=[jax.ShapeDtypeStruct((depth, rows, cols), F32)] * 2,
        in_specs=[pl.BlockSpec(memory_space=SMEM)] * 5 + [pl.BlockSpec(memory_space=VMEM)] * 3,
        out_specs=[pl.BlockSpec(memory_space=VMEM)] * 2,
        scratch_shapes=[pltpu.VMEM((points, cols), BF)],
        compiler_params=pltpu.CompilerParams(vmem_limit_bytes=20 * MIB),
        cost_estimate=pl.CostEstimate(
            flops=2 * 2 * points * (slots + cols) * cols,
            bytes_accessed=12 * points * cols,
            transcendentals=0,
        ),
        name="join",
    )(core, off_z, frac_z, off_y, frac_y, off_x, frac_x, arrived)


def back_kernel(
    core_ref, table, beside_ref, outer_ref, oth_inner_ref, inner_ref, oth_outer_ref, out_ref
):
    share, _, cols = beside_ref.shape
    core = core_ref[0]
    for half, refs in (
        (core, (beside_ref, outer_ref, oth_inner_ref)),
        (1 - core, (oth_inner_ref, inner_ref, oth_outer_ref)),
    ):
        for n in range(0, share, 2):
            data = [jnp.concatenate([ref[n + k] for ref in refs], axis=0) for k in range(2)]
            both = mm(table[...], jnp.concatenate(data, axis=1))
            out_ref[half, n] = both[:, :cols]
            out_ref[half, n + 1] = both[:, cols:]


def back(core, table, beside, outer, oth_inner, inner, oth_outer, share):
    rows, depth, cols = outer.shape
    slab = pl.BlockSpec((share, depth, cols), lambda i, core: (i, 0, 0))
    points = 2 * depth * rows * cols
    return pl.pallas_call(
        back_kernel,
        out_shape=pltpu.HBM((2, rows, depth, cols), F32),
        grid_spec=pltpu.PrefetchScalarGridSpec(
            num_scalar_prefetch=1,
            grid=(rows // share,),
            in_specs=[pl.BlockSpec(table.shape, lambda i, core: (0, 0))] + [slab] * 5,
            out_specs=pl.BlockSpec((2, share, depth, cols), lambda i, core: (0, i, 0, 0)),
        ),
        compiler_params=pltpu.CompilerParams(vmem_limit_bytes=8 * MIB),
        cost_estimate=pl.CostEstimate(
            flops=2 * points * 3 * depth, bytes_accessed=9 * points, transcendentals=0
        ),
        name="back",
    )(core, table, beside, outer, oth_inner, inner, oth_outer)


PLANE = ("y", "x", "core")
VIEW = ("vh", "vl")
COARSE = ("zh", "vh")
RING = ("zh", "vh", "vl")


def swapped(own):
    return lax.ppermute(own, "core", [(0, 1), (1, 0)])


def from_next(end, chips):
    pairs = []
    for chip in range(chips):
        if chip + 1 < chips:
            pairs.append((chip * 2 + 1, chip * 2 + 2))
        if chip > 0:
            pairs.append((chip * 2, chip * 2 - 1))
    return lax.ppermute(end, PLANE, pairs)


def shards(
    chips,
    cap,
    estimate,
    raw_bricks,
    brick_slab,
    brick_pos,
    off_z,
    frac_z,
    off_y,
    frac_y,
    off_x,
    frac_x,
    psf_z,
    psf_y,
    psf_x,
):
    depth, rows, cols = estimate.shape
    count = raw_bricks.shape[1]
    views = lax.axis_size(VIEW)
    share = rows // views
    core = lax.axis_index("core").astype(I32)
    view = lax.axis_index(VIEW).astype(I32)
    place = core.reshape(1)

    piece = turn(lax.axis_index("vh").astype(I32).reshape(1), estimate, rows // lax.axis_size("vh"))
    own = lax.all_gather(piece, COARSE, axis=0, tiled=True).reshape(2, rows, depth, cols)

    packed = pack(
        brick_slab.reshape(1, count), brick_pos, raw_bricks.reshape(count, -1), cap, chips
    )
    packed = packed.reshape(2 * chips, 2 * cap, -1)
    arrived = lax.all_to_all(packed, PLANE, split_axis=0, concat_axis=0, tiled=True)
    weights = tables(core.reshape(1, 1), psf_z, psf_y, psf_x, depth, rows, cols)
    joined = join(
        cap, rows, depth, core.reshape(1, 1), off_z, frac_z, off_y, frac_y, off_x, frac_x, arrived
    )
    own, weights, joined = lax.optimization_barrier((own, weights, joined))
    az, ay, ax, bz, by, bx = weights
    weights = (az, ay, ax, by, bx)
    joined_inner, joined_outer = joined

    same, flip, first = (lambda c: c), (lambda c: 1 - c), (lambda c: 0)
    oth = swapped(own)
    beside = from_next(pick(place, own), chips)[None]
    inner = middle(place, weights, (oth, same), (own, flip), (oth, flip), joined_inner)
    outer = middle(place, weights, (beside, first), (own, same), (oth, same), joined_outer)
    beside = from_next(outer, chips)
    oth_outer = swapped(outer)
    oth_inner = swapped(inner)
    correction = back(place, bz, beside, outer, oth_inner, inner, oth_outer, share)
    correction = correction.reshape(2 * views, share, depth, cols)
    total = lax.psum_scatter(correction, RING, scatter_dimension=0, tiled=True)
    return finish(view.reshape(1), estimate, total.reshape(share, depth, cols), views)


def solution(mesh):
    devices = mesh.devices
    views, slabs = devices.shape
    names = ("vh", "vl", "y", "x", "zh", "core")
    fine = Mesh(devices.reshape(views // 2, 2, 4, slabs // 16, 2, 2), names)
    gz = ("y", "x", "zh", "core")
    in_specs = (
        P(gz, None, None),
        P(VIEW, gz, None, None, None),
        P(VIEW, gz, None),
        P(VIEW, gz),
    ) + (P(VIEW, None),) * 9
    out_specs = P(gz, VIEW, None)
    return jax.shard_map(
        functools.partial(shards, slabs // 4, 16),
        mesh=fine,
        in_specs=in_specs,
        out_specs=out_specs,
        check_vma=False,
    )
```

```python
import functools

import jax
import jax.numpy as jnp
from jax import lax
from jax.experimental import pallas as pl
from jax.experimental.pallas import tpu as pltpu
from jax.sharding import Mesh
from jax.sharding import PartitionSpec as P


BF = jnp.bfloat16
F32 = jnp.float32
I32 = jnp.int32
VMEM = pltpu.VMEM
SMEM = pltpu.SMEM
MIB = 1 << 20


def iota(shape, dim):
    return lax.broadcasted_iota(I32, shape, dim)


def mm(a, b):
    return jnp.dot(a, b, preferred_element_type=F32)


def mm_nt(a, b):
    return lax.dot_general(a, b, (((1,), (1,)), ((), ())), preferred_element_type=F32)


def pack_kernel(cap, groups, slab_ref, pos_ref, bricks_ref, out_ref):
    count, cells = bricks_ref.shape
    slots = out_ref.shape[0]
    slab = slab_ref[...]
    pos = pos_ref[...]
    slabs = groups * 4
    member = (iota((slabs, count), 0) == slab).astype(BF)
    before = (iota((count, count), 0) < iota((count, count), 1)).astype(BF)
    earlier = mm(member, before)
    order = jnp.sum(earlier * member.astype(F32), axis=0, keepdims=True).astype(I32)
    chip = lax.shift_right_logical(slab, 2)
    half = lax.bitwise_and(lax.shift_right_logical(slab, 1), 1)
    core = lax.bitwise_and(slab, 1)
    slot = ((chip * 2 + core) * 2 + half) * cap + order
    block = lax.shift_right_logical(pos, 6) + 1
    row = lax.bitwise_and(pos, 63)
    which = iota((128, count), 0)
    places = jnp.where(which == 0, block, jnp.where(which == 1, row, 0)).astype(F32).astype(BF)
    step = 128
    for at in range(0, slots, step):
        chosen = (iota((step, count), 0) + at == slot).astype(BF)
        out_ref[at : at + step, :cells] = mm(chosen, bricks_ref[...]).astype(BF)
        out_ref[at : at + step, cells:] = mm_nt(chosen, places).astype(BF)


def pack(slab, pos, bricks, cap, groups):
    count, cells = bricks.shape
    slots = groups * 4 * cap
    return pl.pallas_call(
        functools.partial(pack_kernel, cap, groups),
        out_shape=jax.ShapeDtypeStruct((slots, cells + 128), BF),
        in_specs=[pl.BlockSpec(memory_space=VMEM)] * 3,
        out_specs=pl.BlockSpec(memory_space=VMEM),
        compiler_params=pltpu.CompilerParams(vmem_limit_bytes=16 * MIB),
        cost_estimate=pl.CostEstimate(
            flops=2 * slots * count * cells, bytes_accessed=2 * (count + slots) * cells, transcendentals=0
        ),
        name="pack",
    )(slab, pos, bricks)


def smem_sum(ref):
    total = ref[0, 0]
    for k in range(1, ref.shape[1]):
        total = total + ref[0, k]
    return total


def tap_table(psf_ref, which_tap):
    table = jnp.zeros(which_tap.shape, F32)
    for k in range(psf_ref.shape[1]):
        table = jnp.where(which_tap == k, psf_ref[0, k], table)
    total = jnp.full(which_tap.shape, smem_sum(psf_ref), F32)
    return (table / total).astype(BF)


def z_table(psf_ref, core, depth, direction):
    rows, cols = depth, 3 * depth
    r, c = iota((rows, cols), 0), iota((rows, cols), 1)
    side = (lax.div(c, depth) - 1) * (1 - 2 * core)
    distance = side * depth + lax.rem(c, depth) - r
    half = psf_ref.shape[1] // 2
    return tap_table(psf_ref, direction * distance + half)


def split_row(y, rows):
    half = rows // 2
    return jnp.where(y < half, 2 * y, 2 * (y - half) + 1)


def turn_kernel(view_ref, part_ref, out_ref):
    out_ref[...] = jnp.swapaxes(part_ref[...], 0, 1).astype(BF)


def turn(view, estimate, share):
    depth, _, cols = estimate.shape
    return pl.pallas_call(
        turn_kernel,
        out_shape=jax.ShapeDtypeStruct((share, depth, cols), BF),
        grid_spec=pltpu.PrefetchScalarGridSpec(
            num_scalar_prefetch=1,
            grid=(1,),
            in_specs=[pl.BlockSpec((depth, share, cols), lambda i, view: (0, view[0], 0))],
            out_specs=pl.BlockSpec((share, depth, cols), lambda i, view: (0, 0, 0)),
        ),
        cost_estimate=pl.CostEstimate(
            flops=0, bytes_accessed=6 * depth * share * cols, transcendentals=0
        ),
        name="turn",
    )(view, estimate)


def finish_kernel(views, view_ref, part_ref, total_ref, out_ref):
    out_ref[...] = part_ref[...] * jnp.swapaxes(total_ref[...], 0, 1) / views


def finish(view, estimate, total, views):
    share, depth, cols = total.shape
    return pl.pallas_call(
        functools.partial(finish_kernel, views),
        out_shape=jax.ShapeDtypeStruct((depth, share, cols), F32),
        grid_spec=pltpu.PrefetchScalarGridSpec(
            num_scalar_prefetch=1,
            grid=(1,),
            in_specs=[
                pl.BlockSpec((depth, share, cols), lambda i, view: (0, view[0], 0)),
                pl.BlockSpec((share, depth, cols), lambda i, view: (0, 0, 0)),
            ],
            out_specs=pl.BlockSpec((depth, share, cols), lambda i, view: (0, 0, 0)),
        ),
        cost_estimate=pl.CostEstimate(
            flops=0, bytes_accessed=12 * depth * share * cols, transcendentals=0
        ),
        name="finish",
    )(view, estimate, total)


def twice(table):
    zero = jnp.zeros_like(table)
    top = jnp.concatenate([table, zero], axis=1)
    return jnp.concatenate([top, jnp.concatenate([zero, table], axis=1)], axis=0)


def tables_kernel(
    core_ref, psf_z_ref, psf_y_ref, psf_x_ref, az_ref, ay_ref, ax_ref, bz_ref, by_ref, bx_ref
):
    rows, cols = ay_ref.shape[0], ax_ref.shape[0] // 2
    core = core_ref[0, 0]
    lateral = psf_y_ref.shape[1] // 2
    az_ref[...] = z_table(psf_z_ref, core, az_ref.shape[0], 1)
    bz_ref[...] = z_table(psf_z_ref, core, bz_ref.shape[0], -1)
    line, across = iota((rows, rows), 0), iota((rows, rows), 1)
    ay_ref[...] = tap_table(psf_y_ref, across - split_row(line, rows) + lateral)
    by_ref[...] = tap_table(psf_y_ref, line - split_row(across, rows) + lateral)
    line, across = iota((cols, cols), 0), iota((cols, cols), 1)
    ax_ref[...] = twice(tap_table(psf_x_ref, line - across + lateral))
    bx_ref[...] = twice(tap_table(psf_x_ref, across - line + lateral))


def tables(core, psf_z, psf_y, psf_x, depth, rows, cols):
    shapes = ((depth, 3 * depth), (rows, rows), (2 * cols, 2 * cols))
    return pl.pallas_call(
        tables_kernel,
        out_shape=[jax.ShapeDtypeStruct(shape, BF) for shape in shapes * 2],
        in_specs=[pl.BlockSpec(memory_space=SMEM)] * 4,
        out_specs=[pl.BlockSpec(memory_space=VMEM)] * 6,
        compiler_params=pltpu.CompilerParams(vmem_limit_bytes=4 * MIB),
        name="tables",
    )(core, psf_z, psf_y, psf_x)


def pick_kernel(core_ref, own_ref, out_ref):
    pltpu.sync_copy(own_ref.at[core_ref[0]], out_ref)


def pick(core, own):
    return pl.pallas_call(
        pick_kernel,
        out_shape=jax.ShapeDtypeStruct(own.shape[1:], own.dtype),
        in_specs=[pl.BlockSpec(memory_space=SMEM), pl.BlockSpec(memory_space=pltpu.HBM)],
        out_specs=pl.BlockSpec(memory_space=VMEM),
        compiler_params=pltpu.CompilerParams(vmem_limit_bytes=4 * MIB),
        cost_estimate=pl.CostEstimate(flops=0, bytes_accessed=2 * own.size, transcendentals=0),
        name="pick",
    )(core, own)


def middle_kernel(
    picks,
    core_ref,
    az_ref,
    ay_ref,
    ax_ref,
    by_ref,
    bx_ref,
    one_ref,
    own_ref,
    two_ref,
    joined_ref,
    out_ref,
    mid,
    even,
    odd,
    res,
):
    rows, depth, cols = out_ref.shape
    one_ref, own_ref, two_ref = (
        ref.at[which(core_ref[0])]
        for ref, which in zip((one_ref, own_ref, two_ref), picks, strict=True)
    )

    def column(y):
        return jnp.concatenate([one_ref[y], own_ref[y], two_ref[y]], axis=0)

    def axial(i, carry):
        y = pl.multiple_of(i * 8, 8)
        lines = []
        for n in range(0, 8, 2):
            both = mm(az_ref[...], jnp.concatenate([column(y + n), column(y + n + 1)], axis=1))
            lines += [both[:, :cols], both[:, cols:]]
        mid[:, pl.ds(y, 8), :] = jnp.swapaxes(jnp.stack(lines), 0, 1)
        return carry

    lax.fori_loop(0, rows // 8, axial, 0)

    def at(pair):
        return pl.ds(pl.multiple_of(pair * rows, rows), rows)

    def along_y(i, carry):
        for n in range(4):
            pair = i * 4 + n
            both = jnp.concatenate([mid[2 * pair], mid[2 * pair + 1]], axis=1).astype(BF)
            even[at(pair), :] = mm(ay_ref[...], both).astype(BF)
        return carry

    lax.fori_loop(0, depth // 8, along_y, 0)

    def divide(i, carry):
        pair = 2 * i
        here = pl.ds(pl.multiple_of(pair * rows, 2 * rows), 2 * rows)
        blurred = mm(even[here, :], ax_ref[...])
        left = jnp.concatenate([joined_ref[2 * pair], joined_ref[2 * pair + 2]], axis=0)
        right = jnp.concatenate([joined_ref[2 * pair + 1], joined_ref[2 * pair + 3]], axis=0)
        odd[here, :cols] = (left / blurred[:, :cols]).astype(BF)
        odd[here, cols:] = (right / blurred[:, cols:]).astype(BF)
        return carry

    lax.fori_loop(0, depth // 4, divide, 0)

    def along_y_back(i, carry):
        for n in range(4):
            pair = i * 4 + n
            even[at(pair), :] = mm(by_ref[...], odd[at(pair), :]).astype(BF)
        return carry

    lax.fori_loop(0, depth // 8, along_y_back, 0)

    def along_x_back(i, carry):
        here = pl.ds(pl.multiple_of(i * 4 * rows, 4 * rows), 4 * rows)
        both = mm(even[here, :], bx_ref[...])
        planes = []
        for n in range(4):
            planes += [both[n * rows : (n + 1) * rows, k * cols : (k + 1) * cols] for k in (0, 1)]
        z = pl.multiple_of(i * 8, 8)
        res[:, pl.ds(z, 8), :] = jnp.swapaxes(jnp.stack(planes), 0, 1)
        return carry

    lax.fori_loop(0, depth // 8, along_x_back, 0)
    out_ref[...] = res[...].astype(BF)


def middle(core, weights, one, own, two, joined):
    _, rows, depth, cols = own[0].shape
    points = depth * rows * cols
    half = (depth * rows // 2, 2 * cols)
    whole = pl.BlockSpec(memory_space=VMEM)
    return pl.pallas_call(
        functools.partial(middle_kernel, (one[1], own[1], two[1])),
        out_shape=jax.ShapeDtypeStruct((rows, depth, cols), BF),
        grid_spec=pltpu.PrefetchScalarGridSpec(
            num_scalar_prefetch=1,
            grid=(1,),
            in_specs=[whole] * (len(weights) + 4),
            out_specs=whole,
            scratch_shapes=[
                pltpu.VMEM((depth, rows, cols), F32),
                pltpu.VMEM(half, BF),
                pltpu.VMEM(half, BF),
                pltpu.VMEM((rows, depth, cols), F32),
            ],
        ),
        compiler_params=pltpu.CompilerParams(vmem_limit_bytes=20 * MIB),
        cost_estimate=pl.CostEstimate(
            flops=2 * points * (3 * depth + 2 * rows + 2 * cols),
            bytes_accessed=12 * points,
            transcendentals=0,
        ),
        name="middle",
    )(core, *weights, one[0], own[0], two[0], joined)


def interpolation(off_ref, frac_ref, length):
    table = []
    for a in range(length):
        line = []
        for c in range(length):
            frac = frac_ref[0, c]
            low = jnp.where(off_ref[0, c] == a, 1.0 - frac, 0.0)
            high = jnp.where(off_ref[0, c] + 1 == a, frac, 0.0)
            line.append((low, high))
        table.append(line)
    return table


def rounded(value):
    return value.astype(BF).astype(F32)


def join_kernel(
    cap,
    core_ref,
    off_z_ref,
    frac_z_ref,
    off_y_ref,
    frac_y_ref,
    off_x_ref,
    frac_x_ref,
    arrived_ref,
    inner_ref,
    outer_ref,
    mixed,
):
    sources, _, width = arrived_ref.shape
    cols = off_x_ref.shape[1]
    deep, high = off_z_ref.shape[1], off_y_ref.shape[1]
    cells = deep * high
    depth, rows, _ = inner_ref.shape
    core = core_ref[0, 0]
    spots = rows // high
    blocks = depth // deep
    slots = sources * cap
    source = iota((cols, cols), 0)
    off_x = off_x_ref[...]
    frac_x = frac_x_ref[...]
    table_x = jnp.where(source == off_x, rounded(1.0 - frac_x), 0.0)
    table_x = table_x + jnp.where(source == off_x + 1, rounded(frac_x), 0.0)
    table_x = table_x.astype(BF)
    weights_z = interpolation(off_z_ref, frac_z_ref, deep)
    weights_y = interpolation(off_y_ref, frac_y_ref, high)

    def spread(pair):
        low, up = pair
        return rounded(jnp.full((8, cols), low, F32)) + rounded(jnp.full((8, cols), up, F32))

    wide_z = [[spread(p) for p in line] for line in weights_z]
    wide_y = [[spread(p) for p in line] for line in weights_y]
    lane = iota((8, 128), 1)
    decode = jnp.where(lane == 0, spots, jnp.where(lane == 1, 1, 0)).astype(F32).astype(BF)
    for out_ref, h in ((inner_ref, 1 - core), (outer_ref, core)):
        data = arrived_ref[:, pl.ds(pl.multiple_of(h * cap, cap), cap), :].reshape(slots, width)
        place = mm_nt(decode, data[:, cells * cols :])[:1, :].astype(I32) - spots
        for b in range(blocks):
            chosen = (iota((spots, slots), 0) + b * spots == place).astype(BF)
            placed = mm(chosen, data[:, : cells * cols])
            for c in range(deep):
                for d in range(high):
                    acc = jnp.zeros((spots, cols), F32)
                    for a in range(deep):
                        for e in range(high):
                            weight = rounded(wide_z[a][c] * wide_y[e][d])
                            tile = placed[:, (a * high + e) * cols : (a * high + e + 1) * cols]
                            acc = acc + jnp.tile(weight, (spots // 8, 1)) * tile
                    at = (b * deep + c) * rows + d * spots
                    mixed[at : at + spots, :] = acc.astype(BF)
        out_ref[...] = (0.5 + mm(mixed[...], table_x)).reshape(depth, rows, cols)


def join(cap, rows, depth, core, off_z, frac_z, off_y, frac_y, off_x, frac_x, arrived):
    cols = off_x.shape[1]
    slots = arrived.shape[0] * cap
    points = depth * rows
    return pl.pallas_call(
        functools.partial(join_kernel, cap),
        out_shape=[jax.ShapeDtypeStruct((depth, rows, cols), F32)] * 2,
        in_specs=[pl.BlockSpec(memory_space=SMEM)] * 5 + [pl.BlockSpec(memory_space=VMEM)] * 3,
        out_specs=[pl.BlockSpec(memory_space=VMEM)] * 2,
        scratch_shapes=[pltpu.VMEM((points, cols), BF)],
        compiler_params=pltpu.CompilerParams(vmem_limit_bytes=20 * MIB),
        cost_estimate=pl.CostEstimate(
            flops=2 * 2 * points * (slots + cols) * cols,
            bytes_accessed=12 * points * cols,
            transcendentals=0,
        ),
        name="join",
    )(core, off_z, frac_z, off_y, frac_y, off_x, frac_x, arrived)


def back_kernel(
    core_ref, table, beside_ref, outer_ref, oth_inner_ref, inner_ref, oth_outer_ref, out_ref
):
    share, _, cols = beside_ref.shape
    core = core_ref[0]
    for half, refs in (
        (core, (beside_ref, outer_ref, oth_inner_ref)),
        (1 - core, (oth_inner_ref, inner_ref, oth_outer_ref)),
    ):
        for n in range(0, share, 2):
            data = [jnp.concatenate([ref[n + k] for ref in refs], axis=0) for k in range(2)]
            both = mm(table[...], jnp.concatenate(data, axis=1))
            out_ref[half, n] = both[:, :cols]
            out_ref[half, n + 1] = both[:, cols:]


def back(core, table, beside, outer, oth_inner, inner, oth_outer, share):
    rows, depth, cols = outer.shape
    slab = pl.BlockSpec((share, depth, cols), lambda i, core: (i, 0, 0))
    points = 2 * depth * rows * cols
    return pl.pallas_call(
        back_kernel,
        out_shape=pltpu.HBM((2, rows, depth, cols), F32),
        grid_spec=pltpu.PrefetchScalarGridSpec(
            num_scalar_prefetch=1,
            grid=(rows // share,),
            in_specs=[pl.BlockSpec(table.shape, lambda i, core: (0, 0))] + [slab] * 5,
            out_specs=pl.BlockSpec((2, share, depth, cols), lambda i, core: (0, i, 0, 0)),
        ),
        compiler_params=pltpu.CompilerParams(vmem_limit_bytes=8 * MIB),
        cost_estimate=pl.CostEstimate(
            flops=2 * points * 3 * depth, bytes_accessed=9 * points, transcendentals=0
        ),
        name="back",
    )(core, table, beside, outer, oth_inner, inner, oth_outer)


PLANE = ("y", "x", "core")
VIEW = ("vh", "vl")
COARSE = ("zh", "vh")
RING = ("zh", "vh", "vl")


def swapped(own):
    return lax.ppermute(own, "core", [(0, 1), (1, 0)])


def from_next(end, chips):
    pairs = []
    for chip in range(chips):
        if chip + 1 < chips:
            pairs.append((chip * 2 + 1, chip * 2 + 2))
        if chip > 0:
            pairs.append((chip * 2, chip * 2 - 1))
    return lax.ppermute(end, PLANE, pairs)


def shards(
    chips,
    cap,
    estimate,
    raw_bricks,
    brick_slab,
    brick_pos,
    off_z,
    frac_z,
    off_y,
    frac_y,
    off_x,
    frac_x,
    psf_z,
    psf_y,
    psf_x,
):
    depth, rows, cols = estimate.shape
    count = raw_bricks.shape[1]
    views = lax.axis_size(VIEW)
    share = rows // views
    core = lax.axis_index("core").astype(I32)
    view = lax.axis_index(VIEW).astype(I32)
    place = core.reshape(1)

    piece = turn(lax.axis_index("vh").astype(I32).reshape(1), estimate, rows // lax.axis_size("vh"))
    own = lax.all_gather(piece, COARSE, axis=0, tiled=True).reshape(2, rows, depth, cols)

    packed = pack(
        brick_slab.reshape(1, count), brick_pos, raw_bricks.reshape(count, -1), cap, chips
    )
    packed = packed.reshape(2 * chips, 2 * cap, -1)
    arrived = lax.all_to_all(packed, PLANE, split_axis=0, concat_axis=0, tiled=True)
    weights = tables(core.reshape(1, 1), psf_z, psf_y, psf_x, depth, rows, cols)
    joined = join(
        cap, rows, depth, core.reshape(1, 1), off_z, frac_z, off_y, frac_y, off_x, frac_x, arrived
    )
    own, weights, joined = lax.optimization_barrier((own, weights, joined))
    az, ay, ax, bz, by, bx = weights
    weights = (az, ay, ax, by, bx)
    joined_inner, joined_outer = joined

    same, flip, first = (lambda c: c), (lambda c: 1 - c), (lambda c: 0)
    oth = swapped(own)
    beside = from_next(pick(place, own), chips)[None]
    inner = middle(place, weights, (oth, same), (own, flip), (oth, flip), joined_inner)
    outer = middle(place, weights, (beside, first), (own, same), (oth, same), joined_outer)
    beside = from_next(outer, chips)
    oth_outer = swapped(outer)
    oth_inner = swapped(inner)
    correction = back(place, bz, beside, outer, oth_inner, inner, oth_outer, share)
    correction = correction.reshape(2 * views, share, depth, cols)
    total = lax.psum_scatter(correction, RING, scatter_dimension=0, tiled=True)
    return finish(view.reshape(1), estimate, total.reshape(share, depth, cols), views)


def solution(mesh):
    devices = mesh.devices
    views, slabs = devices.shape
    names = ("vh", "vl", "y", "x", "zh", "core")
    fine = Mesh(devices.reshape(views // 2, 2, 4, slabs // 16, 2, 2), names)
    gz = ("y", "x", "zh", "core")
    in_specs = (
        P(gz, None, None),
        P(VIEW, gz, None, None, None),
        P(VIEW, gz, None),
        P(VIEW, gz),
    ) + (P(VIEW, None),) * 9
    out_specs = P(gz, VIEW, None)
    return jax.shard_map(
        functools.partial(shards, slabs // 4, 16),
        mesh=fine,
        in_specs=in_specs,
        out_specs=out_specs,
        check_vma=False,
    )
```
